128 devices in a mesh: ckpt: 8 (over x, z_lo), shard: 16 (over y, z_hi, core).
Axes of the slice: x: 4, y: 4, z: 4 (z_hi: 2, z_lo: 2; z = z_hi * 2 + z_lo), core: 2. Of those that a mesh axis runs over, the one named last changes fastest.
Arguments:
- activations: bfloat16 [8, 2048, 2560], P('ckpt', 'shard'), may hold values from -20 to 20
- loss_mask: int32 [8, 2048], P('ckpt', 'shard'), may hold values from 0 to 1
- gradients: bfloat16 [8, 2048, 14336], P('ckpt', 'shard'), may hold values from -20 to 20
- slabs: bfloat16 [8, 2560, 14336], P('ckpt', None, 'shard'), may hold values from -6 to 6
Outputs:
- merged: bfloat16 [2560, 14336], P(None, 'shard')
The draws below stay inside these ranges and needn't reach their ends.
All inputs are finite; a program needn't handle non-finite values.
Results may differ from the reference program's by a relative error of at most 0.0027.
Values may be sent and summed in bfloat16 or wider, within the bound.
No kernel may reach another device: no remote copies, remote signals or barrier semaphores. Data moves between devices by JAX's collectives and lax.ppermute only.
A program may use at most 128 MiB of HBM per device.

```python
import jax
import jax.numpy as jnp
from jax import lax

D = 2560
F = 14336
TOKENS = 2048
CKPTS = 8


def scaled_field(key, width):
    k_main, k_feat, k_tok = jax.random.split(key, 3)
    base = jnp.clip(jax.random.normal(k_main, (CKPTS, TOKENS, width), jnp.float32), -5.0, 5.0)
    feat = jax.random.uniform(k_feat, (CKPTS, 1, width), jnp.float32, -0.8, 0.8)
    tok = jax.random.uniform(k_tok, (CKPTS, TOKENS, 1), jnp.float32, -0.4, 0.4)
    return (base * jnp.exp(feat) * jnp.exp(tok)).astype(jnp.bfloat16)


def draw_activations(key, part):
    return scaled_field(jax.random.fold_in(key, 101), D)


def draw_gradients(key, part):
    return scaled_field(jax.random.fold_in(key, 202), F)


def draw_loss_mask(key, part):
    draws = jax.random.randint(jax.random.fold_in(key, 303), (CKPTS, TOKENS), 0, 1000)
    position = jnp.arange(TOKENS, dtype=jnp.int32)[None, :]
    limit = 250 + 500 * position // TOKENS
    return (draws < limit).astype(jnp.int32)


def level_of(rng, dims, shards, least, largest):
    level, own = 1.0, jax.random.fold_in(rng, 6)
    for dim, blocks in shards:
        steps = jnp.exp(jax.random.uniform(jax.random.fold_in(own, dim), (blocks,), jnp.float32, least / len(shards), largest / len(shards)))
        level = level * jnp.repeat(steps, dims[dim] // blocks).reshape([-1 if axis == dim else 1 for axis in range(len(dims))])
    return level


def bell_draw(key, shape, spread, most, cuts=(), kind=jnp.bfloat16):
    values = spread * jax.random.normal(key, shape, jnp.float32)
    if cuts:
        values = values * level_of(key, shape, cuts, -0.22, 0.18)
    return jnp.clip(values, -most, most).astype(kind)


def setup_inputs(seed: int = 0) -> dict:
    streams_of = jax.random.split(jax.random.key(seed), 5)
    return {
        "activations": draw_activations(jax.random.fold_in(streams_of[4], 71), 0),
        "loss_mask": draw_loss_mask(jax.random.fold_in(streams_of[4], 71), 0),
        "gradients": draw_gradients(jax.random.fold_in(streams_of[4], 71), 0),
        "slabs": bell_draw(streams_of[3], (CKPTS, D, F), 1.0, 6.0, ((0, 8), (2, 16))),
    }


def reference(activations, loss_mask, gradients, slabs):
    tokens_all = activations.shape[1]
    scale = 1.0 / tokens_all

    def accumulate(carry, items):
        acts, mask, grads, slab = items
        xsq = (jnp.square(acts.astype(jnp.float32)) * mask.astype(jnp.float32)[:, None]).astype(jnp.bfloat16)
        gsq = jnp.square(grads.astype(jnp.float32)).astype(jnp.bfloat16)
        fisher = jnp.dot(xsq.T, gsq, preferred_element_type=jnp.float32) * scale
        numerator, denominator = carry
        return (numerator + fisher * slab.astype(jnp.float32), denominator + fisher), None

    start = (jnp.zeros((D, F), jnp.float32), jnp.zeros((D, F), jnp.float32))
    (numerator, denominator), _ = lax.scan(accumulate, start, (activations, loss_mask, gradients, slabs))
    return (numerator / (denominator + 1e-6)).astype(jnp.bfloat16)
```

```python
import functools

import jax
import jax.numpy as jnp
from jax import lax
from jax.experimental import pallas as pl
from jax.experimental.pallas import tpu as pltpu
from jax.sharding import Mesh, PartitionSpec as P

FLIP_A = ((0, 1), (1, 0), (2, 3), (3, 2))
FLIP_B = ((0, 3), (3, 0), (1, 2), (2, 1))
SWAP = ((0, 1), (1, 0))
CKPT_STEP = {"A": ("x", FLIP_A), "B": ("x", FLIP_B), "Z": ("zl", SWAP)}
CODE_BIT = {"A": 0, "B": 1, "Z": 2}

HALVES = 2
GROUPS = ((0, 512), (512, 384))
PARTS = ((0, 64, "ABZ"), (64, 64, "BAZ"), (128, 32, "ZAB"))
BLOCKS = 8


UP, DOWN = 2.0**60, 2.0**-30


def code(v):
    return (v * jnp.abs(v) * UP).astype(jnp.bfloat16)


def decode(w):
    w = w.astype(jnp.float32)
    root = jnp.sqrt(jnp.abs(w)) * DOWN
    return jnp.where(w < 0, -root, root)


def exchange(value, step):
    axis, perm = CKPT_STEP[step]
    return lax.ppermute(value, axis, perm)


def gray(i):
    return i ^ (i >> 1)


def matmul_kernel(scale, col, width, rows, parts, tab, *refs):
    xs, (g_ref, slab_ref), outs, gs = refs[:8], refs[8:10], refs[10:-1], refs[-1]
    r = pl.program_id(0)

    @pl.when(r == 0)
    def _():
        for s in range(16):
            gs[pl.ds(s * 128, 128), :] = g_ref[tab[s]]

    half = rows // 2
    top, bottom = [], []
    for s in range(16):
        zh, a, b, c = s & 1, (s >> 1) & 1, (s >> 2) & 1, s >> 3
        top.append(xs[c * 4 + b][a * 2 + zh, 0])
        bottom.append(xs[c * 4 + 2 + a][b * 2 + zh, 0])
    x = jnp.concatenate([jnp.concatenate(top, axis=1), jnp.concatenate(bottom, axis=1)], axis=0)
    den = jnp.dot(x, gs[...], preferred_element_type=jnp.float32) * scale
    num = den * slab_ref[:, pl.ds(col, width)].astype(jnp.float32)
    for p, (start, size, order) in enumerate(parts):
        send, keep = outs[2 * p], outs[2 * p + 1]
        b1, b2, b3 = ((r >> CODE_BIT[o]) & 1 for o in order)
        pos = b2 * 2 + b3
        n, d = num[start : start + size], den[start : start + size]

        @pl.when(b1 == 1)
        def _():
            send[pos, 0] = code(n)
            send[pos, 1] = code(d)

        @pl.when(b1 == 0)
        def _():
            keep[pos, 0] = n
            keep[pos, 1] = d


def fisher_parts(tab, xs, g, slab, h, col, width, tokens):
    rows = xs[0].shape[2] * 2
    half = rows // 2
    out_shape, out_specs = [], []
    for _, size, _ in PARTS:
        for dt in (jnp.bfloat16, jnp.float32):
            shape = (4, 2, size, width)
            out_shape.append(jax.ShapeDtypeStruct(shape, dt))
            out_specs.append(pl.BlockSpec(shape, lambda r, t: (0, 0, 0, 0)))
    grid_spec = pltpu.PrefetchScalarGridSpec(
        num_scalar_prefetch=1,
        grid=(BLOCKS,),
        in_specs=[pl.BlockSpec((4, 1, half, 128), lambda r, t: (0, r ^ t[16], 0, 0))] * 8
        + [
            pl.BlockSpec((16, 128, width), lambda r, t: (0, 0, 0)),
            pl.BlockSpec((rows, slab.shape[1]), lambda r, t: (h * BLOCKS + (r ^ t[16]), 0)),
        ],
        out_specs=out_specs,
        scratch_shapes=[pltpu.VMEM((2048, width), jnp.bfloat16)],
    )
    return pl.pallas_call(
        functools.partial(matmul_kernel, 1.0 / tokens, col, width, rows, PARTS),
        grid_spec=grid_spec,
        out_shape=out_shape,
        compiler_params=pltpu.CompilerParams(
            dimension_semantics=("arbitrary",), vmem_limit_bytes=48 * 1024 * 1024
        ),
    )(tab, *xs, g, slab)


def reduce_part(send, keep, order):
    for step, b in enumerate(order):
        got = exchange(send, b)
        total = keep + decode(got)
        if step == 2:
            return (total[0, 0] / (total[0, 1] + 1e-6)).astype(jnp.bfloat16)
        n = total.shape[0] // 2
        keep, send = total[:n], code(total[n:])


def gather_part(mine, order):
    have = mine[None]
    for b in (order[2], order[1]):
        have = jnp.concatenate([have, exchange(have, b)], axis=0)
    return have, exchange(have, order[0])


def place_kernel(row0, rows, col, width, parts, tab, *refs):
    pieces, out, sems = refs[: 2 * len(parts)], refs[-2], refs[-1]
    copies = []
    for p, (start, size, order) in enumerate(parts):
        for b1 in range(2):
            for pos in range(4):
                r = (b1 << CODE_BIT[order[0]]) | ((pos >> 1) << CODE_BIT[order[1]]) | ((pos & 1) << CODE_BIT[order[2]])
                row = pl.multiple_of(row0 + (tab[16] ^ r) * rows + start, 16)
                copy = pltpu.make_async_copy(
                    pieces[2 * p + b1].at[pos],
                    out.at[pl.ds(row, size), pl.ds(col, width)],
                    sems.at[len(copies)],
                )
                copy.start()
                copies.append(copy)
    for copy in copies:
        copy.wait()


def place(tab, pieces, out, shape, row0, rows, col, width):
    operands = list(pieces) + ([] if out is None else [out])
    return pl.pallas_call(
        functools.partial(place_kernel, row0, rows, col, width, PARTS),
        grid_spec=pltpu.PrefetchScalarGridSpec(
            num_scalar_prefetch=1,
            grid=(1,),
            in_specs=[pl.BlockSpec(memory_space=pl.ANY)] * len(operands),
            out_specs=pl.BlockSpec(memory_space=pl.ANY),
            scratch_shapes=[pltpu.SemaphoreType.DMA((8 * len(PARTS),))],
        ),
        out_shape=jax.ShapeDtypeStruct(shape, jnp.bfloat16),
        input_output_aliases={} if out is None else {len(operands): 0},
    )(tab, *operands)


def gather_tokens(block):
    half = block.shape[1] // 2
    other = lax.ppermute(block, "zh", SWAP)
    both = jnp.stack([block, other])
    u, v = both[:, :, :half], both[:, :, half:]
    u4 = jnp.concatenate([u, lax.ppermute(u, "y", FLIP_A)], axis=0)
    v4 = jnp.concatenate([v, lax.ppermute(v, "y", FLIP_B)], axis=0)
    own = [u4, lax.ppermute(u4, "y", FLIP_B), v4, lax.ppermute(v4, "y", FLIP_A)]
    return own + [lax.ppermute(t, "c", SWAP) for t in own]


def body(activations, loss_mask, gradients, slabs):
    d, f = activations.shape[2], gradients.shape[2]
    tokens = 16 * activations.shape[1]
    slab = slabs[0]
    x, zl = lax.axis_index("x"), lax.axis_index("zl")
    y, zh, c = lax.axis_index("y"), lax.axis_index("zh"), lax.axis_index("c")
    me = c * 8 + gray(y) * 2 + zh
    src = jnp.arange(16, dtype=jnp.int32) ^ me
    src_y = gray((src >> 1) & 3)
    tab = jnp.concatenate([src_y * 4 + (src & 1) * 2 + (src >> 3), (zl * 4 + gray(x))[None]]).astype(jnp.int32)

    xsq = (jnp.square(activations[0].astype(jnp.float32)) * loss_mask[0].astype(jnp.float32)[:, None]).astype(jnp.bfloat16)
    rows = d // HALVES // BLOCKS
    xt = xsq.T.reshape(HALVES, BLOCKS, rows, 128)
    gsq = jnp.square(gradients[0].astype(jnp.float32)).astype(jnp.bfloat16).reshape(128, 16, f // 16)
    gsq = gsq.transpose(1, 0, 2)
    gs = [lax.all_to_all(gsq[:, :, s : s + w], ("y", "zh", "c"), 0, 0, tiled=True) for s, w in GROUPS]

    out = None
    for h in range(HALVES):
        xs = gather_tokens(xt[h])
        for (col, width), g in zip(GROUPS, gs):
            halves = fisher_parts(tab, xs, g, slab, h, col, width, tokens)
            pieces = []
            for p, (_, _, order) in enumerate(PARTS):
                mine = reduce_part(halves[2 * p], halves[2 * p + 1], order)
                pieces += gather_part(mine, order)
            out = place(tab, pieces, out, (d, f // 16), h * d // HALVES, rows, col, width)
    return out


def solution(mesh):
    fine = Mesh(mesh.devices.reshape(4, 2, 4, 2, 2), ("x", "zl", "y", "zh", "c"))
    ckpt, shard = ("x", "zl"), ("y", "zh", "c")
    in_specs = (P(ckpt, shard, None), P(ckpt, shard), P(ckpt, shard, None), P(ckpt, None, shard))
    return jax.shard_map(body, mesh=fine, in_specs=in_specs, out_specs=P(None, shard), check_vma=False)
```

```python
import functools

import jax
import jax.numpy as jnp
from jax import lax
from jax.experimental import pallas as pl
from jax.experimental.pallas import tpu as pltpu
from jax.sharding import Mesh, PartitionSpec as P

FLIP = {"A": (1, 0, 3, 2), "B": (3, 2, 1, 0)}
BIT = {"A": 0, "B": 1, "Z": 2}
PARTS = ((0, 208, ("ABZ", "BZA")), (208, 112, ("ZAB", "ZAB")))
GROUPS = ((0, 384), (384, 512))
BLOCKS = 8

UP, DOWN = 2.0**60, 2.0**-30


def code(v):
    return (v * jnp.abs(v) * UP).astype(jnp.bfloat16)


def decode(w):
    w = w.astype(jnp.float32)
    root = jnp.sqrt(jnp.abs(w)) * DOWN
    return jnp.where(w < 0, -root, root)


def gray(i):
    return i ^ (i >> 1)


def exchange(value, orders, step):
    perm = []
    for x in range(4):
        for z in range(2):
            for c in range(2):
                bit = orders[c][step]
                to = (x, 1 - z) if bit == "Z" else (FLIP[bit][x], z)
                perm.append((x * 4 + z * 2 + c, to[0] * 4 + to[1] * 2 + c))
    return lax.ppermute(value, ("x", "zl", "c"), perm)


def swap_y(value, flips):
    perm = [(y * 2 + c, FLIP[flips[c]][y] * 2 + c) for y in range(4) for c in range(2)]
    return lax.ppermute(value, ("y", "c"), perm)


def square_kernel(n, g_ref, *outs):
    for j in range(4):
        g = g_ref[:, j * n : (j + 1) * n].astype(jnp.float32)
        g = (g * g).astype(jnp.bfloat16)
        for out, (col, width) in zip(outs, GROUPS):
            out[j] = g[:, col : col + width]


def square_blocks(gradients):
    tokens, f = gradients.shape
    n = f // 16
    return pl.pallas_call(
        functools.partial(square_kernel, n),
        grid=(4,),
        in_specs=[pl.BlockSpec((tokens, 4 * n), lambda i: (0, i))],
        out_specs=[pl.BlockSpec((4, tokens, w), lambda i: (i, 0, 0)) for _, w in GROUPS],
        out_shape=[jax.ShapeDtypeStruct((16, tokens, w), jnp.bfloat16) for _, w in GROUPS],
        compiler_params=pltpu.CompilerParams(vmem_limit_bytes=32 * 1024 * 1024),
    )(gradients)


def matmul_kernel(scale, col, width, rows, tab, *refs):
    xs, (g_ref, slab_ref), outs, gs = refs[:4], refs[4:6], refs[6:-1], refs[-1]
    i = pl.program_id(0)

    @pl.when(i == 0)
    def _():
        for s in range(16):
            gs[pl.ds(s * 128, 128), :] = g_ref[tab[s]]

    x = jnp.concatenate([ref[s] for ref in xs for s in range(4)], axis=1)
    den = jnp.dot(x, gs[...], preferred_element_type=jnp.float32) * scale
    num = den * slab_ref[:, pl.ds(col, width)].astype(jnp.float32)
    for j in range(2):
        r = 2 * i + (j ^ (tab[16] & 1))
        for p, (start, size, _) in enumerate(PARTS):
            send, keep = outs[2 * p], outs[2 * p + 1]
            b1, b2, b3 = ((r >> tab[17 + 3 * p + k]) & 1 for k in range(3))
            pos = b2 * 2 + b3
            at = slice(j * rows + start, j * rows + start + size)
            n, d = num[at], den[at]

            @pl.when(b1 == 1)
            def _():
                send[pos, 0] = code(n)
                send[pos, 1] = code(d)

            @pl.when(b1 == 0)
            def _():
                keep[pos, 0] = n
                keep[pos, 1] = d


def fisher_parts(tab, xs, g, slab, col, width, tokens):
    rows = slab.shape[0] // BLOCKS
    out_shape, out_specs = [], []
    for _, size, _ in PARTS:
        for dt in (jnp.bfloat16, jnp.float32):
            shape = (4, 2, size, width)
            out_shape.append(jax.ShapeDtypeStruct(shape, dt))
            out_specs.append(pl.BlockSpec(shape, lambda i, t: (0, 0, 0, 0)))
    grid_spec = pltpu.PrefetchScalarGridSpec(
        num_scalar_prefetch=1,
        grid=(BLOCKS // 2,),
        in_specs=[pl.BlockSpec((4, 2 * rows, 128), lambda i, t: (0, i ^ (t[16] >> 1), 0))] * 4
        + [
            pl.BlockSpec((16, 128, width), lambda i, t: (0, 0, 0)),
            pl.BlockSpec((2 * rows, slab.shape[1]), lambda i, t: (i ^ (t[16] >> 1), 0)),
        ],
        out_specs=out_specs,
        scratch_shapes=[pltpu.VMEM((2048, width), jnp.bfloat16)],
    )
    return pl.pallas_call(
        functools.partial(matmul_kernel, 1.0 / tokens, col, width, rows),
        grid_spec=grid_spec,
        out_shape=out_shape,
        compiler_params=pltpu.CompilerParams(
            dimension_semantics=("arbitrary",), vmem_limit_bytes=56 * 1024 * 1024
        ),
    )(tab, *xs, g, slab)


def both(values, step):
    values = lax.optimization_barrier(tuple(values))
    got = [exchange(v, orders, step) for v, (_, _, orders) in zip(values, PARTS)]
    return lax.optimization_barrier(tuple(got))


def reduce_chunk(halves, later):
    sends, keeps = halves[0::2], halves[1::2]
    for step in range(3):
        got = both(sends, step)
        if step == 0:
            keeps = [after(k, *later) for k in keeps]
        totals = [k + decode(g) for k, g in zip(keeps, got)]
        if step == 2:
            return [(t[0, 0] / (t[0, 1] + 1e-6)).astype(jnp.bfloat16) for t in totals]
        n = totals[0].shape[0] // 2
        keeps, sends = [t[:n] for t in totals], [code(t[n:]) for t in totals]


def gather_chunk(mine):
    have = [m[None] for m in mine]
    for step in (2, 1):
        have = [jnp.concatenate([h, g], axis=0) for h, g in zip(have, both(have, step))]
    got = both(have, 0)
    return [t for pair in zip(have, got) for t in pair]


def place_kernel(tab, *refs):
    pieces, out = refs[:-1], refs[-1]
    r = pl.program_id(0) ^ tab[16]
    for p, (start, size, _) in enumerate(PARTS):
        b1, b2, b3 = ((r >> tab[17 + 3 * p + k]) & 1 for k in range(3))
        pos = b2 * 2 + b3
        for q, (col, width) in enumerate(GROUPS):
            have, got = pieces[4 * q + 2 * p : 4 * q + 2 * p + 2]
            for b, piece in enumerate((have, got)):

                @pl.when(b1 == b)
                def _():
                    out[pl.ds(start, size), pl.ds(col, width)] = piece[pos]


def place(tab, pieces, d, n):
    return pl.pallas_call(
        place_kernel,
        grid_spec=pltpu.PrefetchScalarGridSpec(
            num_scalar_prefetch=1,
            grid=(BLOCKS,),
            in_specs=[pl.BlockSpec(t.shape, lambda a, _: (0, 0, 0)) for t in pieces],
            out_specs=pl.BlockSpec((d // BLOCKS, n), lambda a, _: (a, 0)),
        ),
        out_shape=jax.ShapeDtypeStruct((d, n), jnp.bfloat16),
        compiler_params=pltpu.CompilerParams(vmem_limit_bytes=40 * 1024 * 1024),
    )(tab, *pieces)


def after(value, *others):
    return lax.optimization_barrier((value, *others))[0]


def gather_tokens(block, squares):
    def to_all(g):
        return lax.all_to_all(g, ("y", "zh", "c"), 0, 0, tiled=True)

    own = block[None]
    other = lax.ppermute(own, "zh", [(0, 1), (1, 0)])
    first = to_all(squares[0])
    pair = jnp.concatenate([after(own, *squares), other], axis=0)
    four = jnp.concatenate([pair, swap_y(pair, "AB")], axis=0)
    four = after(four, first)
    rest = swap_y(four, "BA")
    second = [to_all(after(g, rest)) for g in squares[1:]]
    xs = [four, rest] + [lax.ppermute(t, "c", [(0, 1), (1, 0)]) for t in (four, rest)]
    return xs, [first] + second


def places():
    x, zl = lax.axis_index("x"), lax.axis_index("zl")
    y, zh, c = lax.axis_index("y"), lax.axis_index("zh"), lax.axis_index("c")
    j = jnp.arange(16, dtype=jnp.int32)
    core = c ^ (j >> 3)
    b1, b2 = (j >> 1) & 1, (j >> 2) & 1
    flips = jnp.where(core == 0, b1 + 2 * b2, b2 + 2 * b1)
    src = gray(gray(y) ^ flips) * 4 + (zh ^ (j & 1)) * 2 + core
    shifts = []
    for _, _, (first, second) in PARTS:
        for k in range(3):
            shifts.append(jnp.where(c == 0, BIT[first[k]], BIT[second[k]]))
    rest = jnp.stack([zl * 4 + gray(x)] + shifts)
    return jnp.concatenate([src, rest]).astype(jnp.int32)


def body(activations, loss_mask, gradients, slabs):
    d, f = activations.shape[2], gradients.shape[2]
    tokens = 16 * activations.shape[1]
    slab = slabs[0]
    tab = places()
    xsq = (jnp.square(activations[0].astype(jnp.float32)) * loss_mask[0].astype(jnp.float32)[:, None]).astype(jnp.bfloat16)
    xs, gs = gather_tokens(xsq.T, square_blocks(gradients[0]))
    chunks = [fisher_parts(tab, xs, g, slab, col, width, tokens) for (col, width), g in zip(GROUPS, gs)]
    pieces = []
    for i, halves in enumerate(chunks):
        later = chunks[i + 1][0::2] if i + 1 < len(chunks) else []
        pieces += gather_chunk(reduce_chunk(halves, later))
    return place(tab, pieces, d, f // 16)


def solution(mesh):
    fine = Mesh(mesh.devices.reshape(4, 2, 4, 2, 2), ("x", "zl", "y", "zh", "c"))
    ckpt, shard = ("x", "zl"), ("y", "zh", "c")
    in_specs = (P(ckpt, shard, None), P(ckpt, shard), P(ckpt, shard, None), P(ckpt, None, shard))
    return jax.shard_map(body, mesh=fine, in_specs=in_specs, out_specs=P(None, shard), check_vma=False)
```

```python
import functools

import jax
import jax.numpy as jnp
from jax import lax
from jax.experimental import pallas as pl
from jax.experimental.pallas import tpu as pltpu
from jax.sharding import Mesh, PartitionSpec as P

FLIP = {"A": (1, 0, 3, 2), "B": (3, 2, 1, 0)}
BIT = {"A": 0, "B": 1, "Z": 2}
BLOCKS = 8
ORDERS = (("ABZ", "BZA"), ("ABZ", "BZA"), ("ZAB", "ABZ"), ("BZA", "ZAB"))
EVENTS = (
    "m0 +0 m1 +1 -0 +0 h m2 +2 m3 +3 -1 +1 -0 +0 -2 +2 -1 +1 -3 +3 -0 +0 -2 +2 -1 +1 -0 +0 -3 +3 "
    "-2 +2 -1 +1 -3 +3 -0 -2 +2 -1 p -3 +3 -2 -3"
)

GROUPS = ((0, 512), (512, 384))
ENDS = ((0, 0), (0, 1), (1, 0), (0, 2), (0, 3), (1, 1), (0, 4), (1, 2), (1, 3), (0, 5), (1, 4), (1, 5))

UP, DOWN = 2.0**60, 2.0**-30


def code(v):
    return (v * jnp.abs(v) * UP).astype(jnp.bfloat16)


def decode(w):
    w = w.astype(jnp.float32)
    root = jnp.sqrt(jnp.abs(w)) * DOWN
    return jnp.where(w < 0, -root, root)


def gray(i):
    return i ^ (i >> 1)


def exchange(value, orders, step):
    perm = []
    for x in range(4):
        for z in range(2):
            for c in range(2):
                bit = orders[c][step]
                to = (x, 1 - z) if bit == "Z" else (FLIP[bit][x], z)
                perm.append((x * 4 + z * 2 + c, to[0] * 4 + to[1] * 2 + c))
    return lax.ppermute(value, ("x", "zl", "c"), perm)


def swap_y(value, flips):
    perm = [(y * 2 + c, FLIP[flips[c]][y] * 2 + c) for y in range(4) for c in range(2)]
    return lax.ppermute(value, ("y", "c"), perm)


def square_kernel(n, g_ref, *outs):
    for j in range(4):
        g = g_ref[:, j * n : (j + 1) * n].astype(jnp.float32)
        g = (g * g).astype(jnp.bfloat16)
        for out, (col, width) in zip(outs, GROUPS):
            out[j] = g[:, col : col + width]


def square_blocks(gradients):
    tokens, f = gradients.shape
    n = f // 16
    return pl.pallas_call(
        functools.partial(square_kernel, n),
        grid=(4,),
        in_specs=[pl.BlockSpec((tokens, 4 * n), lambda i: (0, i))],
        out_specs=[pl.BlockSpec((4, tokens, w), lambda i: (i, 0, 0)) for _, w in GROUPS],
        out_shape=[jax.ShapeDtypeStruct((16, tokens, w), jnp.bfloat16) for _, w in GROUPS],
        compiler_params=pltpu.CompilerParams(vmem_limit_bytes=32 * 1024 * 1024),
    )(gradients)


def bits(r, tab, chunk):
    return tuple((r >> tab[17 + 3 * chunk + k]) & 1 for k in range(3))


def matmul_kernel(scale, chunk, rows, tab, *refs):
    xs, g_ref, slab_ref, send, keep, gs = refs[:4], *refs[4:]
    i = pl.program_id(0)
    col, width = GROUPS[chunk % 2]

    @pl.when(i == 0)
    def _():
        for s in range(16):
            gs[pl.ds(s * 128, 128), :] = g_ref[tab[s]]

    x = jnp.concatenate([ref[s] for ref in xs for s in range(4)], axis=1)
    den = jnp.dot(x, gs[...], preferred_element_type=jnp.float32) * scale
    num = den * slab_ref[:, pl.ds(col, width)].astype(jnp.float32)
    for j in range(4):
        b1, b2, b3 = bits(4 * i + (j ^ (tab[16] & 3)), tab, chunk)
        pos = b2 * 2 + b3
        n, d = num[j * rows : (j + 1) * rows], den[j * rows : (j + 1) * rows]

        @pl.when(b1 == 1)
        def _():
            send[0, pos] = code(n)
            send[1, pos] = code(d)

        @pl.when(b1 == 0)
        def _():
            keep[0, pos] = n
            keep[1, pos] = d


def fisher_chunk(tab, xs, g, slab, chunk, tokens):
    rows = xs[0].shape[1] // BLOCKS
    base, width = 2 * (chunk // 2), g.shape[2]
    shape = (2, 4, rows, width)
    grid_spec = pltpu.PrefetchScalarGridSpec(
        num_scalar_prefetch=1,
        grid=(2,),
        in_specs=[pl.BlockSpec((4, 4 * rows, 128), lambda i, t: (0, i ^ (t[16] >> 2), 0))] * 4
        + [
            pl.BlockSpec(g.shape, lambda i, t: (0, 0, 0)),
            pl.BlockSpec((4 * rows, slab.shape[1]), lambda i, t: (base + (i ^ (t[16] >> 2)), 0)),
        ],
        out_specs=[pl.BlockSpec(shape, lambda i, t: (0, 0, 0, 0))] * 2,
        scratch_shapes=[pltpu.VMEM((2048, width), jnp.bfloat16)],
    )
    return pl.pallas_call(
        functools.partial(matmul_kernel, 1.0 / tokens, chunk, rows),
        grid_spec=grid_spec,
        out_shape=[jax.ShapeDtypeStruct(shape, dt) for dt in (jnp.bfloat16, jnp.float32)],
        compiler_params=pltpu.CompilerParams(
            dimension_semantics=("arbitrary",), vmem_limit_bytes=56 * 1024 * 1024
        ),
    )(tab, *xs, g, slab)


def chunk_steps(send, keep):
    for step in range(2):
        got = yield send, step
        total = keep + decode(got)
        n = total.shape[1] // 2
        if step == 0:
            keep, send = total[:, :n], code(total[:, n:])
    send = code(total)
    got = yield send, 2
    total = decode(send) + jnp.flip(decode(got), 1)
    have = (total[0] / (total[1] + 1e-6)).astype(jnp.bfloat16)
    got = yield have, 1
    have = jnp.concatenate([have, got], axis=0)
    got = yield have, 0
    yield [have, got], None


def place_kernel(half, tab, *refs):
    pieces, out = refs[:4], refs[-1]
    r = pl.program_id(0) ^ tab[16]
    for q, (col, width) in enumerate(GROUPS):
        b1, b2, b3 = bits(r, tab, 2 * half + q)
        for b in range(2):

            @pl.when(b1 == b)
            def _():
                out[:, pl.ds(col, width)] = pieces[2 * q + b][b2 * 2 + b3]


def place(tab, pieces, half, out, shape):
    old = [] if out is None else [out]
    return pl.pallas_call(
        functools.partial(place_kernel, half),
        grid_spec=pltpu.PrefetchScalarGridSpec(
            num_scalar_prefetch=1,
            grid=(BLOCKS,),
            in_specs=[pl.BlockSpec(t.shape, lambda a, _: (0, 0, 0)) for t in pieces]
            + [pl.BlockSpec(memory_space=pl.ANY) for _ in old],
            out_specs=pl.BlockSpec((pieces[0].shape[1], shape[1]), lambda a, _: (half * BLOCKS + a, 0)),
        ),
        out_shape=jax.ShapeDtypeStruct(shape, jnp.bfloat16),
        input_output_aliases={5: 0} if old else {},
        compiler_params=pltpu.CompilerParams(vmem_limit_bytes=40 * 1024 * 1024),
    )(tab, *pieces, *old)


def after(value, *others):
    return lax.optimization_barrier((value, *others))[0]


def swap_core(value):
    return lax.ppermute(value, "c", [(0, 1), (1, 0)])


def all_chunks(xt, squares, multiply, put):
    def to_all(g):
        return lax.all_to_all(g, ("y", "zh", "c"), 0, 0, tiled=True)

    half = xt.shape[0] // 2
    other = lax.ppermute(xt, "zh", [(0, 1), (1, 0)])
    g0 = to_all(squares[0])
    xt = after(xt, *squares)
    pair0, pair1 = (jnp.stack([xt[m : m + half], other[m : m + half]]) for m in (0, half))
    four0 = after(jnp.concatenate([pair0, swap_y(pair0, "AB")], axis=0), g0)
    g1 = to_all(after(squares[1], four0))
    pair1 = after(pair1, four0)
    rest0 = swap_y(four0, "BA")
    four1 = after(jnp.concatenate([pair1, swap_y(pair1, "AB")], axis=0), rest0)
    rest1 = swap_y(four1, "BA")
    xs = {0: [four0, rest0, swap_core(four0), swap_core(rest0)]}
    gs = (g0, g1)
    runs, ready, flying, gate, out = {}, {}, {}, [four1], None
    for event in EVENTS.split():
        kind, i = event[0], int(event[1:] or 0)
        if kind == "h":
            rest1 = after(rest1, *gate)
            xs[1] = [four1, rest1, swap_core(four1), swap_core(rest1)]
        elif kind == "p":
            out = put(0, ready[0][0] + ready[1][0], None)
            gate = [out[:16, :128]]
        elif kind == "m":
            send, keep = multiply(i, xs[i // 2], after(gs[i % 2], *gate))
            runs[i] = chunk_steps(send, keep)
            ready[i] = next(runs[i])
            gate = [send]
        elif kind == "+":
            send = ready[i][0]
            if gate[0] is not send:
                send = after(send, *gate)
            flying[i] = exchange(send, ORDERS[i], ready[i][1])
            gate = [send]
        else:
            ready[i] = runs[i].send(after(flying[i], *gate))
    return put(1, ready[2][0] + ready[3][0], out)


def places():
    x, zl = lax.axis_index("x"), lax.axis_index("zl")
    y, zh, c = lax.axis_index("y"), lax.axis_index("zh"), lax.axis_index("c")
    j = jnp.arange(16, dtype=jnp.int32)
    core = c ^ (j >> 3)
    b1, b2 = (j >> 1) & 1, (j >> 2) & 1
    flips = jnp.where(core == 0, b1 + 2 * b2, b2 + 2 * b1)
    src = gray(gray(y) ^ flips) * 4 + (zh ^ (j & 1)) * 2 + core
    shifts = []
    for first, second in ORDERS:
        for k in range(3):
            shifts.append(jnp.where(c == 0, BIT[first[k]], BIT[second[k]]))
    rest = jnp.stack([zl * 4 + gray(x)] + shifts)
    return jnp.concatenate([src, rest]).astype(jnp.int32)


def body(activations, loss_mask, gradients, slabs):
    d, f = activations.shape[2], gradients.shape[2]
    tokens = 16 * activations.shape[1]
    slab = slabs[0]
    tab = places()
    xsq = (jnp.square(activations[0].astype(jnp.float32)) * loss_mask[0].astype(jnp.float32)[:, None]).astype(jnp.bfloat16)
    squares = square_blocks(gradients[0])
    return all_chunks(
        xsq.T,
        squares,
        lambda i, xs, g: fisher_chunk(tab, xs, g, slab, i, tokens),
        lambda h, pieces, out: place(tab, pieces, h, out, (d, f // 16)),
    )


def solution(mesh):
    fine = Mesh(mesh.devices.reshape(4, 2, 4, 2, 2), ("x", "zl", "y", "zh", "c"))
    ckpt, shard = ("x", "zl"), ("y", "zh", "c")
    in_specs = (P(ckpt, shard, None), P(ckpt, shard), P(ckpt, shard, None), P(ckpt, None, shard))
    return jax.shard_map(body, mesh=fine, in_specs=in_specs, out_specs=P(None, shard), check_vma=False)
```

```python
import functools

import jax
import jax.numpy as jnp
from jax import lax
from jax.experimental import pallas as pl
from jax.experimental.pallas import tpu as pltpu
from jax.sharding import Mesh, PartitionSpec as P

FLIP = {"A": (1, 0, 3, 2), "B": (3, 2, 1, 0)}
BIT = {"A": 0, "B": 1, "Z": 2}
ORDERS = (("ABZ", "BZA"), ("ZAB", "ZAB"))
BLOCKS = 8
CHUNKS = ((112, 48), (112, 48))
EVENTS = (
    ("+", 0), ("m", 1), ("+", 1), ("-", 0), ("+", 0), ("-", 0), ("+", 0), ("-", 1),
    ("+", 1), ("-", 1), ("+", 1), ("-", 0), ("+", 0), ("-", 1), ("+", 1), ("-", 0),
    ("+", 0), ("-", 1), ("+", 1), ("-", 0), ("-", 1),
)

GROUPS = ((0, 512), (512, 384))
ENDS = ((0, 0), (0, 1), (1, 0), (0, 2), (0, 3), (1, 1), (0, 4), (1, 2), (1, 3), (0, 5), (1, 4), (1, 5))

UP, DOWN = 2.0**60, 2.0**-30


def code(v):
    return (v * jnp.abs(v) * UP).astype(jnp.bfloat16)


def code_last(v):
    return (v * v * v * UP).astype(jnp.bfloat16)


def decode_last(w):
    w = w.astype(jnp.float32)
    root = jnp.exp2(jnp.log2(jnp.abs(w)) * (1.0 / 3.0)) * 2.0**-20
    return jnp.where(w < 0, -root, root)


def decode(w):
    w = w.astype(jnp.float32)
    root = jnp.sqrt(jnp.abs(w)) * DOWN
    return jnp.where(w < 0, -root, root)


def gray(i):
    return i ^ (i >> 1)


def exchange(value, orders, step):
    perm = []
    for x in range(4):
        for z in range(2):
            for c in range(2):
                bit = orders[c][step]
                to = (x, 1 - z) if bit == "Z" else (FLIP[bit][x], z)
                perm.append((x * 4 + z * 2 + c, to[0] * 4 + to[1] * 2 + c))
    return lax.ppermute(value, ("x", "zl", "c"), perm)


def swap_y(value, flips):
    perm = [(y * 2 + c, FLIP[flips[c]][y] * 2 + c) for y in range(4) for c in range(2)]
    return lax.ppermute(value, ("y", "c"), perm)


def square_kernel(n, g_ref, *outs):
    for j in range(4):
        g = g_ref[:, j * n : (j + 1) * n].astype(jnp.float32)
        g = (g * g).astype(jnp.bfloat16)
        for out, (col, width) in zip(outs, GROUPS):
            out[j] = g[:, col : col + width]


def square_blocks(gradients):
    tokens, f = gradients.shape
    n = f // 16
    return pl.pallas_call(
        functools.partial(square_kernel, n),
        grid=(4,),
        in_specs=[pl.BlockSpec((tokens, 4 * n), lambda i: (0, i))],
        out_specs=[pl.BlockSpec((4, tokens, w), lambda i: (i, 0, 0)) for _, w in GROUPS],
        out_shape=[jax.ShapeDtypeStruct((16, tokens, w), jnp.bfloat16) for _, w in GROUPS],
        compiler_params=pltpu.CompilerParams(vmem_limit_bytes=32 * 1024 * 1024),
    )(gradients)


def bits(r, tab, part):
    return tuple((r >> tab[17 + 3 * part + k]) & 1 for k in range(3))


def matmul_kernel(scale, parts, tab, *refs):
    xs, g_refs, slab_ref, outs, gs = refs[:4], refs[4:6], refs[6], refs[7:-1], refs[-1]
    i = pl.program_id(0)

    @pl.when(i == 0)
    def _():
        for s in range(16):
            for g_ref, (col, size) in zip(g_refs, GROUPS):
                gs[pl.ds(s * 128, 128), pl.ds(col, size)] = g_ref[tab[s]]

    x = jnp.concatenate([ref[s] for ref in xs for s in range(4)], axis=1)
    den = jnp.dot(x, gs[...], preferred_element_type=jnp.float32) * scale
    num = den * slab_ref[...].astype(jnp.float32)
    start = 0
    for j in range(4):
        r = 4 * i + (j ^ (tab[16] & 3))
        for p, size in enumerate(parts):
            send, keep = outs[2 * p], outs[2 * p + 1]
            b1, b2, b3 = bits(r, tab, p)
            pos = b2 * 2 + b3
            n, d = num[start : start + size], den[start : start + size]
            start += size

            @pl.when(b1 == 1)
            def _():
                send[0, pos] = code(n)
                send[1, pos] = code(d)

            @pl.when(b1 == 0)
            def _():
                keep[0, pos] = n
                keep[1, pos] = d


def fisher_parts(tab, xs, gs, slab, chunk, tokens):
    width = slab.shape[1]
    parts = CHUNKS[chunk]
    rows = 4 * sum(parts)
    base = BLOCKS * sum(sum(c) for c in CHUNKS[:chunk]) // rows
    out_shape, out_specs = [], []
    for size in parts:
        for dt in (jnp.bfloat16, jnp.float32):
            shape = (2, 4, size, width)
            out_shape.append(jax.ShapeDtypeStruct(shape, dt))
            out_specs.append(pl.BlockSpec(shape, lambda i, t: (0, 0, 0, 0)))
    grid_spec = pltpu.PrefetchScalarGridSpec(
        num_scalar_prefetch=1,
        grid=(2,),
        in_specs=[pl.BlockSpec((4, rows, 128), lambda i, t: (0, i ^ (t[16] >> 2), 0))] * 4
        + [pl.BlockSpec((16, 128, w), lambda i, t: (0, 0, 0)) for _, w in GROUPS]
        + [pl.BlockSpec((rows, width), lambda i, t: (base + (i ^ (t[16] >> 2)), 0))],
        out_specs=out_specs,
        scratch_shapes=[pltpu.VMEM((2048, width), jnp.bfloat16)],
    )
    return pl.pallas_call(
        functools.partial(matmul_kernel, 1.0 / tokens, parts),
        grid_spec=grid_spec,
        out_shape=out_shape,
        compiler_params=pltpu.CompilerParams(
            dimension_semantics=("arbitrary",), vmem_limit_bytes=60 * 1024 * 1024
        ),
    )(tab, *xs, *gs, slab)


def chunk_steps(halves):
    sends, keeps = halves[0::2], halves[1::2]
    for step in range(2):
        got = yield sends, step
        totals = [k + decode(g) for k, g in zip(keeps, got)]
        n = totals[0].shape[1] // 2
        if step == 0:
            keeps, sends = [t[:, :n] for t in totals], [code(t[:, n:]) for t in totals]
    sends = [code_last(t) for t in totals]
    got = yield sends, 2
    totals = [decode_last(v) + jnp.flip(decode_last(g), 1) for v, g in zip(sends, got)]
    have = [(t[0] / (t[1] + 1e-6)).astype(jnp.bfloat16) for t in totals]
    got = yield have, 1
    have = [jnp.concatenate([h, g], axis=0) for h, g in zip(have, got)]
    got = yield have, 0
    yield [t for pair in zip(have, got) for t in pair], None


def exchange_chunks(chunks):
    runs = [chunk_steps(halves) for halves in chunks]
    ready, flying = {i: next(run) for i, run in enumerate(runs)}, {}
    gate = []
    for kind, i in EVENTS:
        if kind == "+":
            sends, step = ready[i]
            if gate:
                sends = list(lax.optimization_barrier((*sends, *gate))[: len(ORDERS)])
            flying[i] = [exchange(v, orders, step) for v, orders in zip(sends, ORDERS)]
            gate = sends
        elif kind == "-":
            got = flying[i]
            if gate:
                got = lax.optimization_barrier((*got, *gate))[: len(ORDERS)]
            ready[i] = runs[i].send(got)
        else:
            gate = list(chunks[i][1::2])
    return [t for i in range(len(chunks)) for t in ready[i][0]]


def place_kernel(tab, *refs):
    pieces, out = refs[:-1], refs[-1]
    r = pl.program_id(0) ^ tab[16]
    for i, parts in enumerate(CHUNKS):
        start = 0
        for p, size in enumerate(parts):
            b1, b2, b3 = bits(r, tab, p)
            for b in range(2):

                @pl.when(b1 == b)
                def _():
                    out[i, pl.ds(start, size), :] = pieces[4 * i + 2 * p + b][b2 * 2 + b3]

            start += size


def place(tab, pieces, d, n):
    chunks = len(CHUNKS)
    return pl.pallas_call(
        place_kernel,
        grid_spec=pltpu.PrefetchScalarGridSpec(
            num_scalar_prefetch=1,
            grid=(BLOCKS,),
            in_specs=[pl.BlockSpec(t.shape, lambda a, _: (0, 0, 0)) for t in pieces],
            out_specs=pl.BlockSpec((chunks, sum(CHUNKS[0]), n), lambda a, _: (0, a, 0)),
        ),
        out_shape=jax.ShapeDtypeStruct((chunks, d // chunks, n), jnp.bfloat16),
        compiler_params=pltpu.CompilerParams(vmem_limit_bytes=40 * 1024 * 1024),
    )(tab, *pieces).reshape(d, n)


def after(value, *others):
    return lax.optimization_barrier((value, *others))[0]


def swap_core(value):
    return lax.ppermute(value, "c", [(0, 1), (1, 0)])


def all_pieces(xt, squares, multiply):
    def to_all(g):
        return lax.all_to_all(g, ("y", "zh", "c"), 0, 0, tiled=True)

    cuts = [BLOCKS * sum(sum(c) for c in CHUNKS[:i]) for i in range(len(CHUNKS) + 1)]
    other = lax.ppermute(xt, "zh", [(0, 1), (1, 0)])
    g0 = to_all(squares[0])
    xt = after(xt, *squares)
    pair0, pair1 = (jnp.stack([xt[m:n], other[m:n]]) for m, n in zip(cuts, cuts[1:]))
    four0 = after(jnp.concatenate([pair0, swap_y(pair0, "AB")], axis=0), g0)
    g1 = to_all(after(squares[1], four0))
    pair1 = after(pair1, four0)
    rest0 = swap_y(four0, "BA")
    four1 = after(jnp.concatenate([pair1, swap_y(pair1, "AB")], axis=0), rest0)
    rest1 = swap_y(four1, "BA")
    first = multiply(0, [four0, rest0, swap_core(four0), swap_core(rest0)], [g0, g1])
    rest1 = after(rest1, *first[0::2])
    second = multiply(1, [four1, rest1, swap_core(four1), swap_core(rest1)], [g0, g1])
    return [first, second]


def places():
    x, zl = lax.axis_index("x"), lax.axis_index("zl")
    y, zh, c = lax.axis_index("y"), lax.axis_index("zh"), lax.axis_index("c")
    j = jnp.arange(16, dtype=jnp.int32)
    core = c ^ (j >> 3)
    b1, b2 = (j >> 1) & 1, (j >> 2) & 1
    flips = jnp.where(core == 0, b1 + 2 * b2, b2 + 2 * b1)
    src = gray(gray(y) ^ flips) * 4 + (zh ^ (j & 1)) * 2 + core
    shifts = []
    for first, second in ORDERS:
        for k in range(3):
            shifts.append(jnp.where(c == 0, BIT[first[k]], BIT[second[k]]))
    rest = jnp.stack([zl * 4 + gray(x)] + shifts)
    return jnp.concatenate([src, rest]).astype(jnp.int32)


def body(activations, loss_mask, gradients, slabs):
    d, f = activations.shape[2], gradients.shape[2]
    tokens = 16 * activations.shape[1]
    slab = slabs[0]
    tab = places()
    xsq = (jnp.square(activations[0].astype(jnp.float32)) * loss_mask[0].astype(jnp.float32)[:, None]).astype(jnp.bfloat16)
    squares = square_blocks(gradients[0])
    chunks = all_pieces(xsq.T, squares, lambda i, xs, gs: fisher_parts(tab, xs, gs, slab, i, tokens))
    return place(tab, exchange_chunks(chunks), d, f // 16)


def solution(mesh):
    fine = Mesh(mesh.devices.reshape(4, 2, 4, 2, 2), ("x", "zl", "y", "zh", "c"))
    ckpt, shard = ("x", "zl"), ("y", "zh", "c")
    in_specs = (P(ckpt, shard, None), P(ckpt, shard), P(ckpt, shard, None), P(ckpt, None, shard))
    return jax.shard_map(body, mesh=fine, in_specs=in_specs, out_specs=P(None, shard), check_vma=False)
```
